32 devices in a mesh: section: 4 (over y, x), strip: 4 (over z), mirror: 2 (over core).
Axes of the slice: x: 2, y: 2, z: 4, core: 2. Of those that a mesh axis runs over, the one named last changes fastest.
Arguments:
- grad_top: bfloat16 [2, 4, 32, 16, 256], P('mirror', None, 'strip'), may hold values from -6 to 6
- acts: bfloat16 [2, 4, 4, 32, 16, 256], P('mirror', 'section', None, 'strip'), may hold values from -6 to 6
- masks: int32 [2, 4, 4, 32, 16, 256], P('mirror', 'section', None, 'strip'), may hold values 0 or 1
- kernels: bfloat16 [2, 4, 3, 3, 256, 256], P('mirror', 'section'), as said below
Outputs:
- input_grads: bfloat16 [2, 4, 4, 32, 16, 256], P('mirror', 'section', None, 'strip')
- kernel_grads: float32 [2, 4, 2304, 256], P('mirror', 'section', 'strip')
The draws below stay inside these ranges and needn't reach their ends.
Inputs may be any that keep to these rules, and one draw needn't show every extreme that they name: kernels[1, s] equals kernels[0, 3 - s]: both replicas hold the same layers, in opposite order over the section positions.
All inputs are finite; a program needn't handle non-finite values. No bound on the sum of `masks` on one device may be relied on, other than what follows from the above.
Results may differ from the reference program's by a relative error of at most 0.015.
Values may be sent and summed in bfloat16 or wider, within the bound.
No kernel may reach another device: no remote copies, remote signals or barrier semaphores. Data moves between devices by JAX's collectives and lax.ppermute only.
A program may use at most 64 MiB of HBM per device.

```python
import math
import jax
import jax.numpy as jnp
from jax import lax

C = 256
MICRO = 4
WD = 16
LAYERS = 4
H = 32


def draw_kernels(key, part):
    factor = (36.0 * C) ** (-0.5)
    drawn = jax.random.normal(key, (LAYERS, 3, 3, C, C), jnp.float32) * factor
    return jnp.stack([drawn, drawn[::-1]]).astype(jnp.bfloat16)


def place_ends(array, rng, smallest, high):
    shape = array.shape
    place = [jax.random.randint(jax.random.fold_in(rng, axis), (), 0, shape[axis]) for axis in range(len(shape))]
    array = array.at[tuple(place)].set(smallest)
    longest = shape.index(max(shape))
    place[longest] = (place[longest] + 1) % shape[longest]
    return array.at[tuple(place)].set(high)


def block_levels(stream_key, dims, cuts, least, top_value):
    factor_of = 1.0
    for dim, blocks in cuts:
        heights = jax.random.uniform(jax.random.fold_in(jax.random.fold_in(stream_key, 6), dim), (blocks,), jnp.float32, least / len(cuts), top_value / len(cuts))
        factor_of = factor_of * jnp.repeat(jnp.exp(heights), dims[dim] // blocks).reshape((-1,) + (1,) * (len(dims) - 1 - dim))
    return factor_of


def normal_values(key, extent, width, most, split=(), dtype=jnp.bfloat16):
    values = jax.random.normal(key, extent, jnp.float32) * width
    if len(split) > 0:
        values = block_levels(key, extent, split, -0.22, 0.18) * values
    return jnp.clip(values, min=-most, max=most).astype(dtype)


def setup_inputs(seed: int = 0) -> dict:
    key_list = jax.random.split(jax.random.key(seed), 5)
    grad_top = normal_values(key_list[0], (2, MICRO, H, WD, C), 1.0, 6.0, ((0, 2), (2, 4)))
    acts = normal_values(key_list[1], (2, LAYERS, MICRO, H, WD, C), 1.0, 6.0, ((0, 2), (1, 4), (3, 4)))
    masks = place_ends((jax.random.randint(key_list[2], (2, LAYERS, MICRO, H, WD, C), 0, 2) < 1).astype(jnp.int32), jax.random.fold_in(key_list[2], 1), 0, 1)
    kernels = draw_kernels(jax.random.fold_in(key_list[4], 71), 0)
    return dict(grad_top=grad_top, acts=acts, masks=masks, kernels=kernels)


def unfold(padded, height, tile_width, flipped):
    pieces = []
    for row_shift in range(3):
        for col_shift in range(3):
            if flipped:
                row_start = 2 - row_shift
                col_start = 2 - col_shift
            else:
                row_start = row_shift
                col_start = col_shift
            pieces.append(padded[row_start:row_start + height, col_start:col_start + tile_width])
    stacked = jnp.concatenate(pieces, axis=-1)
    return stacked.reshape(height * tile_width, stacked.shape[-1])

def layer_back(grad_out, inputs, relu_mask, kernel):
    height, tile_width, channels = grad_out.shape
    grad_pre = (grad_out.astype(jnp.float32) * relu_mask.astype(jnp.float32)).astype(jnp.bfloat16)
    pad_config = ((1, 1), (1, 1), (0, 0))
    input_patch = unfold(jnp.pad(inputs, pad_config), height, tile_width, False)
    grad_patch = unfold(jnp.pad(grad_pre, pad_config), height, tile_width, True)
    kernel_grad = lax.dot_general(input_patch, grad_pre.reshape(height * tile_width, channels), (((0,), (0,)), ((), ())), preferred_element_type=jnp.float32)
    kernel_t = jnp.transpose(kernel, (0, 1, 3, 2)).reshape(9 * channels, channels)
    branch = jnp.dot(grad_patch, kernel_t, preferred_element_type=jnp.float32)
    grad_in = grad_out.astype(jnp.float32) + branch.reshape(height, tile_width, channels)
    return (grad_in.astype(jnp.bfloat16), kernel_grad)

def reference(grad_top, acts, masks, kernels):
    height = grad_top.shape[2]
    tile_width = grad_top.shape[3]
    channels = grad_top.shape[4]
    totals = [jnp.zeros((9 * channels, channels), jnp.float32) for layer_id in range(LAYERS)]
    collected = [[[None] * MICRO for position in range(LAYERS)] for replica in range(2)]
    for replica in range(2):
        for micro_id in range(MICRO):
            grad_out = grad_top[replica, micro_id]
            for layer_id in range(LAYERS - 1, -1, -1):
                position = layer_id if replica == 0 else LAYERS - 1 - layer_id
                grad_out, kernel_grad = layer_back(grad_out, acts[replica, position, micro_id], masks[replica, position, micro_id], kernels[replica, position])
                totals[layer_id] = totals[layer_id] + kernel_grad
                collected[replica][position][micro_id] = grad_out
    factor = 1.0 / math.sqrt(2.0 * MICRO * height * tile_width)
    input_grads = jnp.stack([jnp.stack([jnp.stack(collected[replica][position]) for position in range(LAYERS)]) for replica in range(2)])
    kernel_rows = []
    for replica in range(2):
        per_section = []
        for position in range(LAYERS):
            layer_id = position if replica == 0 else LAYERS - 1 - position
            per_section.append(totals[layer_id] * factor)
        kernel_rows.append(jnp.stack(per_section))
    kernel_grads = jnp.stack(kernel_rows)
    return (input_grads, kernel_grads)
```

```python
import math

import jax
import jax.numpy as jnp
from jax import lax
from jax.sharding import PartitionSpec as P


def with_halo(block, sides, width):
    for axis, dim in sides:
        count = lax.axis_size(axis)
        forward = [(i, i + 1) for i in range(count - 1)]
        backward = [(target, source) for source, target in forward]
        low = lax.ppermute(
            lax.slice_in_dim(block, block.shape[dim] - width, None, axis=dim), axis, forward
        )
        high = lax.ppermute(lax.slice_in_dim(block, 0, width, axis=dim), axis, backward)
        block = jnp.concatenate([low, block, high], axis=dim)
    return block


def from_behind(block, axis, distance):
    devices = range(lax.axis_size(axis))
    route = [(i - distance, i) for i in devices if i - distance in devices]
    return lax.ppermute(block, axis, route)


def swapped(shard, axis, bit):
    return lax.ppermute(shard, axis, [(i, i ^ 1 << bit) for i in range(lax.axis_size(axis))])


def unfold(padded, height, tile_width, flipped):
    pieces = []
    for row_shift in range(3):
        for col_shift in range(3):
            if flipped:
                row_start = 2 - row_shift
                col_start = 2 - col_shift
            else:
                row_start = row_shift
                col_start = col_shift
            pieces.append(
                padded[row_start : row_start + height, col_start : col_start + tile_width]
            )
    stacked = jnp.concatenate(pieces, axis=-1)
    return stacked.reshape(height * tile_width, stacked.shape[-1])


def pipelined(grad_top, acts, masks, kernels):
    sections = lax.axis_size("section")
    strips = lax.axis_size("strip")
    section_id = lax.axis_index("section")
    mirror_id = lax.axis_index("mirror")
    layer_id = jnp.where(mirror_id == 0, section_id, sections - 1 - section_id)
    delay_ticks = sections - 1 - layer_id
    top_grads = grad_top[0]
    inputs_all = acts[0, 0]
    masks_all = masks[0, 0]
    kernel = kernels[0, 0]
    micros, tile_rows, tile_width, channels = inputs_all.shape
    kernel_t = jnp.transpose(kernel, (0, 1, 3, 2)).reshape(9 * channels, channels)
    width_pad = ((0, 0), (1, 1), (0, 0))

    def compute(operands):
        grad_rim, input_rim, grad_out, kernel_acc = operands
        grad_pre = grad_rim[1:-1]
        input_patch = unfold(jnp.pad(input_rim, width_pad), tile_rows, tile_width, False)
        grad_patch = unfold(jnp.pad(grad_rim, width_pad), tile_rows, tile_width, True)
        kernel_acc = kernel_acc + lax.dot_general(
            input_patch,
            grad_pre.reshape(tile_rows * tile_width, channels),
            (((0,), (0,)), ((), ())),
            preferred_element_type=jnp.float32,
        )
        branch = jnp.dot(grad_patch, kernel_t, preferred_element_type=jnp.float32)
        grad_in = grad_out.astype(jnp.float32) + branch.reshape(tile_rows, tile_width, channels)
        return (grad_in.astype(jnp.bfloat16), kernel_acc)

    def skipped(operands):
        return (jnp.zeros_like(operands[2]), operands[3])

    def backward(tick_id, carried):
        incoming, kernel_acc, results = carried
        micro_id = tick_id - delay_ticks
        active = jnp.logical_and(micro_id >= 0, micro_id < micros)
        clipped = jnp.clip(micro_id, 0, micros - 1)
        from_top = lax.dynamic_index_in_dim(top_grads, clipped, 0, keepdims=False)
        grad_out = jnp.where(layer_id == sections - 1, from_top, incoming)
        relu_mask = lax.dynamic_index_in_dim(masks_all, clipped, 0, keepdims=False)
        grad_pre = (grad_out.astype(jnp.float32) * relu_mask.astype(jnp.float32)).astype(
            jnp.bfloat16
        )
        inputs = lax.dynamic_index_in_dim(inputs_all, clipped, 0, keepdims=False)
        rimmed = with_halo(jnp.stack([grad_pre, inputs]), (("strip", 1),), 1)
        grad_rim = rimmed[0]
        input_rim = rimmed[1]
        grad_in, kernel_acc = lax.cond(
            active, compute, skipped, (grad_rim, input_rim, grad_out, kernel_acc)
        )
        current = lax.dynamic_index_in_dim(results, clipped, 0, keepdims=False)
        stored = jnp.where(active, grad_in, current)
        results = lax.dynamic_update_index_in_dim(results, stored, clipped, 0)
        from_below = from_behind(grad_in, "section", -1)
        higher = from_behind(grad_in, "section", 1)
        incoming = jnp.where(mirror_id == 0, from_below, higher)
        return (incoming, kernel_acc, results)

    initial = (
        jnp.zeros((tile_rows, tile_width, channels), jnp.bfloat16),
        jnp.zeros((9 * channels, channels), jnp.float32),
        jnp.zeros((micros, tile_rows, tile_width, channels), jnp.bfloat16),
    )
    incoming, kernel_acc, results = lax.fori_loop(0, micros + sections - 1, backward, initial)
    share_rows = 9 * channels // strips
    own_share = lax.psum_scatter(kernel_acc, "strip", scatter_dimension=0, tiled=True)
    blocks = own_share.reshape(sections, share_rows * channels // sections)
    spread = lax.all_to_all(blocks, "section", split_axis=0, concat_axis=0, tiled=True)
    across = swapped(spread.astype(jnp.bfloat16), "mirror", 0).astype(spread.dtype)
    combined = spread + jnp.flip(across, 0)
    returned = lax.all_to_all(combined, "section", split_axis=0, concat_axis=0, tiled=True)
    summed_share = returned.reshape(share_rows, channels)
    factor = 1.0 / math.sqrt(2.0 * micros * tile_rows * strips * tile_width)
    kernel_grads = (summed_share * factor)[None, None]
    input_grads = results[None, None]
    return (input_grads, kernel_grads)


AXES = ("section", "strip", "mirror")


def folded(grad_top, acts, masks, kernels):
    sections = lax.axis_size("section")
    strips = lax.axis_size("strip")
    section_id = lax.axis_index("section")
    strip_id = lax.axis_index("strip")
    mirror_id = lax.axis_index("mirror")
    layer_id = jnp.where(mirror_id == 0, section_id, sections - 1 - section_id)
    stage = sections - 1 - layer_id
    upper = layer_id >= sections // 2
    bf16 = jnp.bfloat16
    rim = sections

    def layer_of(s, m):
        return s if m == 0 else sections - 1 - s

    def place(layer, m):
        return (layer if m == 0 else sections - 1 - layer, m)

    def flat(s, z, m):
        return (s * strips + z) * 2 + m

    def owner(s, m):
        return (s, m) if layer_of(s, m) >= sections // 2 else (sections - 1 - s, 1 - m)

    cells = [(s, m) for s in range(sections) for m in range(2)]

    def fetched(block, shift, cyclic, only_lower=False, own_data=False):
        route = []
        for s, m in cells:
            if only_lower and owner(s, m) == (s, m):
                continue
            source = (s, m) if own_data else owner(s, m)
            for z in range(strips):
                if cyclic or 0 <= z - shift < strips:
                    route.append((flat(source[0], (z - shift) % strips, source[1]), flat(s, z, m)))
        return lax.ppermute(block, AXES, route)

    def advanced(block):
        route = []
        for s, m in cells:
            layer = layer_of(s, m)
            replica = m if layer >= sections // 2 else 1 - m
            below = (layer - 1) % sections
            target = place(below, replica if below >= sections // 2 else 1 - replica)
            for z in range(strips):
                route.append((flat(s, z, m), flat(target[0], z, target[1])))
        return lax.ppermute(block, AXES, route)

    def partnered(block):
        route = [
            (flat(s, z, m), flat(sections - 1 - s, z, 1 - m)) for s, m in cells for z in range(strips)
        ]
        return lax.ppermute(block, AXES, route)

    top_grads = grad_top[0]
    inputs_all = acts[0, 0]
    masks_all = masks[0, 0].astype(bf16)
    micros, tile_rows, tile_width, channels = inputs_all.shape
    kernel_t = jnp.transpose(kernels[0, 0], (0, 1, 3, 2)).reshape(9 * channels, channels)
    pixels = tile_rows * tile_width
    rows = 9 * channels // strips

    both = jnp.stack([top_grads, masks_all])
    low = fetched(both[:, :, tile_rows - rim :], 1, False)
    high = fetched(both[:, :, :rim], -1, False)
    moved = fetched(masks_all, 0, False, only_lower=True)
    masks_mine = jnp.where(upper, masks_all, moved)
    mask_ext = jnp.concatenate([low[1], masks_mine, high[1]], axis=1)
    top_ext = jnp.concatenate([low[0], top_grads, high[0]], axis=1)

    moved_inputs = fetched(inputs_all, 0, False, only_lower=True)
    blocks = [jnp.where(upper, inputs_all, moved_inputs)]
    for d in range(1, strips):
        blocks.append(fetched(inputs_all, d, True))

    def own_rows(j):
        def build(parts):
            first, last = rows * j, rows * (j + 1)
            taps = []
            for d in range(strips):
                above = parts[(d + 1) % strips][:, tile_rows - 1 :]
                below = parts[(d - 1) % strips][:, :1]
                z = (j - d) % strips
                if z == 0:
                    above = jnp.zeros_like(above)
                if z == strips - 1:
                    below = jnp.zeros_like(below)
                tall = jnp.concatenate([above, parts[d], below], axis=1)
                wide = jnp.pad(tall, ((0, 0), (0, 0), (1, 1), (0, 0)))
                pieces = []
                for tap in range(first // channels, (last - 1) // channels + 1):
                    a, b = divmod(tap, 3)
                    left = max(first - tap * channels, 0)
                    right = min(last - tap * channels, channels)
                    pieces.append(wide[:, a : a + tile_rows, b : b + tile_width, left:right])
                taps.append(jnp.concatenate(pieces, axis=-1).reshape(micros, pixels, rows))
            return jnp.concatenate(taps, axis=1)

        return build

    patches = lax.switch(strip_id, [own_rows(j) for j in range(strips)], blocks)

    ext_rows = tile_rows + 2 * rim
    incoming = jnp.zeros((ext_rows, tile_width, channels), bf16)
    kernel_acc = jnp.zeros((rows, channels), jnp.float32)
    outs = []
    ticks = micros + sections - 1
    for tick in range(ticks):
        micro_id = tick - stage
        active = jnp.logical_and(micro_id >= 0, micro_id < micros)
        clipped = jnp.clip(micro_id, 0, micros - 1)
        grad_out = jnp.where(stage == 0, top_ext[min(tick, micros - 1)], incoming)
        relu_mask = lax.dynamic_index_in_dim(mask_ext, clipped, 0, keepdims=False)
        grad_pre = grad_out * jnp.where(active, relu_mask, jnp.zeros_like(relu_mask))
        patch = unfold(jnp.pad(grad_pre, ((1, 1), (1, 1), (0, 0))), ext_rows, tile_width, True)
        branch = jnp.dot(patch, kernel_t, preferred_element_type=jnp.float32)
        grad_in = grad_out.astype(jnp.float32) + branch.reshape(ext_rows, tile_width, channels)
        grad_in = grad_in.astype(bf16)
        outs.append(grad_in[rim : rim + tile_rows])
        if tick + 1 < ticks:
            inner = advanced(grad_in[1:-1])
            incoming = jnp.pad(inner, ((1, 1), (0, 0), (0, 0)))
        centre = grad_pre[rim : rim + tile_rows].reshape(pixels, channels)
        gathered = [centre]
        for d in range(1, strips):
            gathered.append(fetched(centre, d, True, own_data=True))
        kernel_acc = kernel_acc + lax.dot_general(
            lax.dynamic_index_in_dim(patches, clipped, 0, keepdims=False),
            jnp.concatenate(gathered, axis=0),
            (((0,), (0,)), ((), ())),
            preferred_element_type=jnp.float32,
        )

    results = lax.dynamic_slice_in_dim(jnp.stack(outs), stage, micros, axis=0)
    returned = fetched(results, 0, False, only_lower=True)
    input_grads = jnp.where(upper, results, returned)
    across = partnered(kernel_acc.astype(bf16)).astype(jnp.float32)
    factor = 1.0 / math.sqrt(2.0 * micros * tile_rows * strips * tile_width)
    kernel_grads = (kernel_acc + across) * factor
    return (input_grads[None, None], kernel_grads[None, None])


def shards(grad_top, acts, masks, kernels):
    sections = lax.axis_size("section")
    strips = lax.axis_size("strip")
    tile_rows, channels = acts.shape[3], acts.shape[5]
    fits = sections % 2 == 0 and sections <= tile_rows and 9 * channels % strips == 0
    if fits:
        return folded(grad_top, acts, masks, kernels)
    return pipelined(grad_top, acts, masks, kernels)


def solution(mesh):
    return jax.shard_map(
        shards,
        mesh=mesh,
        in_specs=(
            P("mirror", None, "strip", None, None),
            P("mirror", "section", None, "strip", None, None),
            P("mirror", "section", None, "strip", None, None),
            P("mirror", "section", None, None, None, None),
        ),
        out_specs=(
            P("mirror", "section", None, "strip", None, None),
            P("mirror", "section", "strip", None),
        ),
        check_vma=False,
    )
```

```python
import math

import jax
import jax.numpy as jnp
from jax import lax
from jax.sharding import PartitionSpec as P


def with_halo(block, sides, width):
    for axis, dim in sides:
        count = lax.axis_size(axis)
        forward = [(i, i + 1) for i in range(count - 1)]
        backward = [(target, source) for source, target in forward]
        low = lax.ppermute(
            lax.slice_in_dim(block, block.shape[dim] - width, None, axis=dim), axis, forward
        )
        high = lax.ppermute(lax.slice_in_dim(block, 0, width, axis=dim), axis, backward)
        block = jnp.concatenate([low, block, high], axis=dim)
    return block


def from_behind(block, axis, distance):
    devices = range(lax.axis_size(axis))
    route = [(i - distance, i) for i in devices if i - distance in devices]
    return lax.ppermute(block, axis, route)


def swapped(shard, axis, bit):
    return lax.ppermute(shard, axis, [(i, i ^ 1 << bit) for i in range(lax.axis_size(axis))])


def unfold(padded, height, tile_width, flipped):
    pieces = []
    for row_shift in range(3):
        for col_shift in range(3):
            if flipped:
                row_start = 2 - row_shift
                col_start = 2 - col_shift
            else:
                row_start = row_shift
                col_start = col_shift
            pieces.append(
                padded[row_start : row_start + height, col_start : col_start + tile_width]
            )
    stacked = jnp.concatenate(pieces, axis=-1)
    return stacked.reshape(height * tile_width, stacked.shape[-1])


def pipelined(grad_top, acts, masks, kernels):
    sections = lax.axis_size("section")
    strips = lax.axis_size("strip")
    section_id = lax.axis_index("section")
    mirror_id = lax.axis_index("mirror")
    layer_id = jnp.where(mirror_id == 0, section_id, sections - 1 - section_id)
    delay_ticks = sections - 1 - layer_id
    top_grads = grad_top[0]
    inputs_all = acts[0, 0]
    masks_all = masks[0, 0]
    kernel = kernels[0, 0]
    micros, tile_rows, tile_width, channels = inputs_all.shape
    kernel_t = jnp.transpose(kernel, (0, 1, 3, 2)).reshape(9 * channels, channels)
    width_pad = ((0, 0), (1, 1), (0, 0))

    def compute(operands):
        grad_rim, input_rim, grad_out, kernel_acc = operands
        grad_pre = grad_rim[1:-1]
        input_patch = unfold(jnp.pad(input_rim, width_pad), tile_rows, tile_width, False)
        grad_patch = unfold(jnp.pad(grad_rim, width_pad), tile_rows, tile_width, True)
        kernel_acc = kernel_acc + lax.dot_general(
            input_patch,
            grad_pre.reshape(tile_rows * tile_width, channels),
            (((0,), (0,)), ((), ())),
            preferred_element_type=jnp.float32,
        )
        branch = jnp.dot(grad_patch, kernel_t, preferred_element_type=jnp.float32)
        grad_in = grad_out.astype(jnp.float32) + branch.reshape(tile_rows, tile_width, channels)
        return (grad_in.astype(jnp.bfloat16), kernel_acc)

    def skipped(operands):
        return (jnp.zeros_like(operands[2]), operands[3])

    def backward(tick_id, carried):
        incoming, kernel_acc, results = carried
        micro_id = tick_id - delay_ticks
        active = jnp.logical_and(micro_id >= 0, micro_id < micros)
        clipped = jnp.clip(micro_id, 0, micros - 1)
        from_top = lax.dynamic_index_in_dim(top_grads, clipped, 0, keepdims=False)
        grad_out = jnp.where(layer_id == sections - 1, from_top, incoming)
        relu_mask = lax.dynamic_index_in_dim(masks_all, clipped, 0, keepdims=False)
        grad_pre = (grad_out.astype(jnp.float32) * relu_mask.astype(jnp.float32)).astype(
            jnp.bfloat16
        )
        inputs = lax.dynamic_index_in_dim(inputs_all, clipped, 0, keepdims=False)
        rimmed = with_halo(jnp.stack([grad_pre, inputs]), (("strip", 1),), 1)
        grad_rim = rimmed[0]
        input_rim = rimmed[1]
        grad_in, kernel_acc = lax.cond(
            active, compute, skipped, (grad_rim, input_rim, grad_out, kernel_acc)
        )
        current = lax.dynamic_index_in_dim(results, clipped, 0, keepdims=False)
        stored = jnp.where(active, grad_in, current)
        results = lax.dynamic_update_index_in_dim(results, stored, clipped, 0)
        from_below = from_behind(grad_in, "section", -1)
        higher = from_behind(grad_in, "section", 1)
        incoming = jnp.where(mirror_id == 0, from_below, higher)
        return (incoming, kernel_acc, results)

    initial = (
        jnp.zeros((tile_rows, tile_width, channels), jnp.bfloat16),
        jnp.zeros((9 * channels, channels), jnp.float32),
        jnp.zeros((micros, tile_rows, tile_width, channels), jnp.bfloat16),
    )
    _, kernel_acc, results = lax.fori_loop(0, micros + sections - 1, backward, initial)
    share_rows = 9 * channels // strips
    own_share = lax.psum_scatter(kernel_acc, "strip", scatter_dimension=0, tiled=True)
    blocks = own_share.reshape(sections, share_rows * channels // sections)
    spread = lax.all_to_all(blocks, "section", split_axis=0, concat_axis=0, tiled=True)
    across = swapped(spread.astype(jnp.bfloat16), "mirror", 0).astype(spread.dtype)
    combined = spread + jnp.flip(across, 0)
    returned = lax.all_to_all(combined, "section", split_axis=0, concat_axis=0, tiled=True)
    summed_share = returned.reshape(share_rows, channels)
    factor = 1.0 / math.sqrt(2.0 * micros * tile_rows * strips * tile_width)
    kernel_grads = (summed_share * factor)[None, None]
    input_grads = results[None, None]
    return (input_grads, kernel_grads)


AXES = ("section", "strip", "mirror")


def after(value, *others):
    return lax.optimization_barrier((value, *others))[0]


def folded(grad_top, acts, masks, kernels):
    sections = lax.axis_size("section")
    strips = lax.axis_size("strip")
    half = sections // 2
    section_id = lax.axis_index("section")
    strip_id = lax.axis_index("strip")
    mirror_id = lax.axis_index("mirror")
    replica = jnp.where(section_id >= half, 0, 1)
    major = mirror_id == replica
    depth = jnp.where(section_id >= half, sections - 1 - section_id, section_id)
    bf16 = jnp.bfloat16

    def flat(s, z, m):
        return (s * strips + z) * 2 + m

    def is_major(s, m):
        return m == (0 if s >= half else 1)

    cells = [(s, m) for s in range(sections) for m in range(2)]

    def permuted(block, target, wanted=lambda s, m: True):
        route = []
        for s, m in cells:
            if wanted(s, m):
                t, n = target(s, m)
                route.extend((flat(s, z, m), flat(t, z, n)) for z in range(strips))
        return lax.ppermute(block, AXES, route)

    def mirrored(block):
        return lax.ppermute(block, "mirror", [(0, 1), (1, 0)])

    def partnered(block, lower):
        return permuted(
            block,
            lambda s, m: (sections - 1 - s, 1 - m),
            lambda s, m: is_major(s, m) != bool(lower),
        )

    def cored(block, lower):
        return permuted(block, lambda s, m: (s, 1 - m), lambda s, m: is_major(s, m) == bool(lower))

    def minor_to_major(block):
        return permuted(block, lambda s, m: (sections - 1 - s, m), lambda s, m: not is_major(s, m))

    def stripped(block, step, wanted=lambda s, m: True):
        route = [
            (flat(s, z, m), flat(s, z ^ step, m))
            for s, m in cells
            if wanted(s, m)
            for z in range(strips)
        ]
        return lax.ppermute(block, AXES, route)

    def hopped(block, position):
        inner = [min(q, sections - 1 - q) for q in (position, position + 1)]
        swap = {inner[0]: inner[1], inner[1]: inner[0]}
        swap.update({sections - 1 - a: sections - 1 - b for a, b in list(swap.items())})
        return permuted(block, lambda s, m: (swap[s], m), lambda s, m: s in swap)

    even = strip_id % 2 == 0

    def rims(first, last):
        near = [(z, z + 1) for z in range(0, strips - 1, 2)]
        far = [(z, z + 1) for z in range(1, strips - 1, 2)]
        near, far = [pairs + [(b, a) for a, b in pairs] for pairs in (near, far)]
        from_near = lax.ppermute(jnp.where(even, last, first), "strip", near)
        from_far = lax.ppermute(jnp.where(even, first, last), "strip", far)
        return jnp.where(even, from_far, from_near), jnp.where(even, from_near, from_far)

    def across_strips(block):
        return jnp.concatenate([block, stripped(block, 1)])

    top_grads = grad_top[0]
    inputs_all = acts[0, 0]
    masks_int = masks[0, 0]
    micros, tile_rows, tile_width, channels = inputs_all.shape
    count = micros // 2
    pixels = tile_rows * tile_width
    rows = 9 * channels // strips

    mine = jnp.stack([top_grads[:count], masks_int[:count].astype(bf16)])
    theirs = jnp.stack([top_grads[count:], masks_int[count:].astype(bf16)])
    mine = jnp.where(major, mine, mirrored(theirs))
    low, high = rims(mine[:, :, :sections], mine[:, :, tile_rows - sections :])
    top_ext, high_masks = jnp.concatenate([low, mine, high], axis=2)

    own_kernel = jnp.transpose(kernels[0, 0], (0, 1, 3, 2)).reshape(9 * channels, channels)
    other_kernel = mirrored(own_kernel)
    high_kernel = jnp.where(major, own_kernel, other_kernel)
    low_kernel = jnp.where(major, other_kernel, own_kernel)

    low_all = after(jnp.stack([masks_int.astype(bf16), inputs_all]), mine)
    moved = jnp.where(major, minor_to_major(low_all[:, :count]), partnered(low_all[:, count:], 1))
    given_inputs = mirrored(after(inputs_all[count:], mine))
    high_inputs = jnp.where(major, inputs_all[:count], given_inputs)

    def later_rims():
        block = jnp.concatenate([moved, high_inputs[None]])
        first = jnp.concatenate([block[0, :, :half], block[1, :, :1], block[2, :, :1]], axis=1)
        end = tile_rows
        last = jnp.concatenate(
            [block[0, :, end - half :], block[1, :, end - 1 :], block[2, :, end - 1 :]], axis=1
        )
        low, high = rims(first, last)
        low_masks = jnp.concatenate([low[:, :half], block[0], high[:, :half]], axis=1)
        low_inputs = [low[:, half : half + 1], block[1], high[:, half : half + 1]]
        high_inputs_ext = [low[:, half + 1 :], block[2], high[:, half + 1 :]]
        inputs = jnp.concatenate(
            [jnp.concatenate(high_inputs_ext, axis=1), jnp.concatenate(low_inputs, axis=1)]
        )
        return low_masks, across_strips(inputs[None])

    column, upper_strip = strip_id % 2, strip_id // 2

    def unfolded(tall):
        wide = jnp.pad(tall, ((0, 0), (0, 0), (0, 0), (1, 1), (0, 0)))

        def tap(index):
            a, b = divmod(index, 3)
            return wide[:, :, a : a + tile_rows, b : b + tile_width]

        pieces = [
            jnp.where(column == 1, tap(first + 2), tap(first)) for first in (0, 1, 2, 4, 5, 6)
        ]
        joined = jnp.concatenate(pieces, axis=-1).reshape(2, 2, count * pixels, 6 * channels)
        return joined.swapaxes(0, 1).reshape(2, 2 * count * pixels, 6 * channels)

    def kept_rows(taps):
        start = column * (channels // 4)
        near = lax.dynamic_slice_in_dim(taps, start, rows)
        far = lax.dynamic_slice_in_dim(taps[3 * channels :], start + channels // 2, rows)
        return near, far

    def layer_back(grad_out, mask, kernel):
        height = grad_out.shape[0] - 2
        grad_pre = grad_out * mask
        padded = jnp.pad(grad_pre, ((0, 0), (1, 1), (0, 0)))
        patch = unfold(padded, height, tile_width, True)
        branch = jnp.dot(patch, kernel, preferred_element_type=jnp.float32)
        grad_in = grad_out[1:-1].astype(jnp.float32) + branch.reshape(height, tile_width, channels)
        return grad_in.astype(bf16), grad_pre

    grads = [top_ext[k] for k in range(count)]
    pres = [[None] * count for _ in range(sections)]
    outs = [[None] * count for _ in range(sections)]
    low_masks = inputs = None
    for position in range(sections):
        for k in range(count):
            lower = position >= half
            trim = position - half if lower else position
            mask = (low_masks if lower else high_masks)[k]
            mask = mask[trim : mask.shape[0] - trim]
            kernel = low_kernel if lower else high_kernel
            grad_in, grad_pre = layer_back(grads[k], mask, kernel)
            rim = sections - position
            pres[position][k] = grad_pre[rim : rim + tile_rows]
            outs[position][k] = grad_in[rim - 1 : rim - 1 + tile_rows]
            grads[k] = grad_in
            if position + 1 < sections and position + 1 != half:
                hop = hopped(grad_in, position)
                grads[k] = hop if position else jnp.where(depth == 0, grad_in, hop)
        if position == 0:
            low_masks, inputs = later_rims()

    def at_depth(pieces):
        chosen = pieces[0]
        for q in range(1, half):
            chosen = jnp.where(depth == q, pieces[q], chosen)
        return chosen

    def side(table, lower, k):
        return at_depth([table[sections - 1 - q if lower else q][k] for q in range(half)])

    results = [jnp.stack([side(outs, lower, k) for k in range(count)]) for lower in range(2)]
    given = mirrored(jnp.where(major, results[1], results[0]))
    kept = jnp.concatenate([results[0], given])
    returned = partnered(jnp.concatenate([given, results[1]]), 1)
    input_grads = jnp.where(major, kept, returned)

    patches = unfolded(inputs)
    sums = []
    for lower in range(2):
        holds = lambda s, m: is_major(s, m) != bool(lower)
        block = jnp.stack([side(pres, lower, k) for k in range(count)])[None]
        own = lax.dot_general(
            patches[lower],
            across_strips(block).reshape(-1, channels),
            (((0,), (0,)), ((), ())),
            preferred_element_type=jnp.float32,
        )
        own = jnp.stack(kept_rows(own))
        own = own + cored(own.astype(bf16), lower).astype(jnp.float32)
        other = jnp.where(upper_strip == 0, own[1], own[0]).astype(bf16)
        own = jnp.where(upper_strip == 0, own[0], own[1])
        own = own + stripped(other, 2, holds).astype(jnp.float32)
        sums.append(own + partnered(own.astype(bf16), lower).astype(jnp.float32))
    factor = 1.0 / math.sqrt(2.0 * micros * tile_rows * strips * tile_width)
    kernel_grads = jnp.where(major, sums[0], sums[1]) * factor
    return (input_grads[None, None], kernel_grads[None, None])


def shards(grad_top, acts, masks, kernels):
    sections = lax.axis_size("section")
    strips = lax.axis_size("strip")
    tile_rows, channels = acts.shape[3], acts.shape[5]
    paired = sections % 2 == 0 and acts.shape[2] % 2 == 0 and strips == 4
    if paired and sections <= tile_rows and 9 * channels % strips == 0:
        return folded(grad_top, acts, masks, kernels)
    return pipelined(grad_top, acts, masks, kernels)


def solution(mesh):
    return mapped(mesh)


def mapped(mesh):
    return jax.shard_map(
        shards,
        mesh=mesh,
        in_specs=(
            P("mirror", None, "strip", None, None),
            P("mirror", "section", None, "strip", None, None),
            P("mirror", "section", None, "strip", None, None),
            P("mirror", "section", None, None, None, None),
        ),
        out_specs=(
            P("mirror", "section", None, "strip", None, None),
            P("mirror", "section", "strip", None),
        ),
        check_vma=False,
    )
```

```python
import math

import jax
import jax.numpy as jnp
from jax import lax
from jax.sharding import PartitionSpec as P


def with_halo(block, sides, width):
    for axis, dim in sides:
        count = lax.axis_size(axis)
        forward = [(i, i + 1) for i in range(count - 1)]
        backward = [(target, source) for source, target in forward]
        low = lax.ppermute(
            lax.slice_in_dim(block, block.shape[dim] - width, None, axis=dim), axis, forward
        )
        high = lax.ppermute(lax.slice_in_dim(block, 0, width, axis=dim), axis, backward)
        block = jnp.concatenate([low, block, high], axis=dim)
    return block


def from_behind(block, axis, distance):
    devices = range(lax.axis_size(axis))
    route = [(i - distance, i) for i in devices if i - distance in devices]
    return lax.ppermute(block, axis, route)


def swapped(shard, axis, bit):
    return lax.ppermute(shard, axis, [(i, i ^ 1 << bit) for i in range(lax.axis_size(axis))])


def unfold(padded, height, tile_width, flipped):
    pieces = []
    for row_shift in range(3):
        for col_shift in range(3):
            if flipped:
                row_start = 2 - row_shift
                col_start = 2 - col_shift
            else:
                row_start = row_shift
                col_start = col_shift
            pieces.append(
                padded[row_start : row_start + height, col_start : col_start + tile_width]
            )
    stacked = jnp.concatenate(pieces, axis=-1)
    return stacked.reshape(height * tile_width, stacked.shape[-1])


def pipelined(grad_top, acts, masks, kernels):
    sections = lax.axis_size("section")
    strips = lax.axis_size("strip")
    section_id = lax.axis_index("section")
    mirror_id = lax.axis_index("mirror")
    layer_id = jnp.where(mirror_id == 0, section_id, sections - 1 - section_id)
    delay_ticks = sections - 1 - layer_id
    top_grads = grad_top[0]
    inputs_all = acts[0, 0]
    masks_all = masks[0, 0]
    kernel = kernels[0, 0]
    micros, tile_rows, tile_width, channels = inputs_all.shape
    kernel_t = jnp.transpose(kernel, (0, 1, 3, 2)).reshape(9 * channels, channels)
    width_pad = ((0, 0), (1, 1), (0, 0))

    def compute(operands):
        grad_rim, input_rim, grad_out, kernel_acc = operands
        grad_pre = grad_rim[1:-1]
        input_patch = unfold(jnp.pad(input_rim, width_pad), tile_rows, tile_width, False)
        grad_patch = unfold(jnp.pad(grad_rim, width_pad), tile_rows, tile_width, True)
        kernel_acc = kernel_acc + lax.dot_general(
            input_patch,
            grad_pre.reshape(tile_rows * tile_width, channels),
            (((0,), (0,)), ((), ())),
            preferred_element_type=jnp.float32,
        )
        branch = jnp.dot(grad_patch, kernel_t, preferred_element_type=jnp.float32)
        grad_in = grad_out.astype(jnp.float32) + branch.reshape(tile_rows, tile_width, channels)
        return (grad_in.astype(jnp.bfloat16), kernel_acc)

    def skipped(operands):
        return (jnp.zeros_like(operands[2]), operands[3])

    def backward(tick_id, carried):
        incoming, kernel_acc, results = carried
        micro_id = tick_id - delay_ticks
        active = jnp.logical_and(micro_id >= 0, micro_id < micros)
        clipped = jnp.clip(micro_id, 0, micros - 1)
        from_top = lax.dynamic_index_in_dim(top_grads, clipped, 0, keepdims=False)
        grad_out = jnp.where(layer_id == sections - 1, from_top, incoming)
        relu_mask = lax.dynamic_index_in_dim(masks_all, clipped, 0, keepdims=False)
        grad_pre = (grad_out.astype(jnp.float32) * relu_mask.astype(jnp.float32)).astype(
            jnp.bfloat16
        )
        inputs = lax.dynamic_index_in_dim(inputs_all, clipped, 0, keepdims=False)
        rimmed = with_halo(jnp.stack([grad_pre, inputs]), (("strip", 1),), 1)
        grad_rim = rimmed[0]
        input_rim = rimmed[1]
        grad_in, kernel_acc = lax.cond(
            active, compute, skipped, (grad_rim, input_rim, grad_out, kernel_acc)
        )
        current = lax.dynamic_index_in_dim(results, clipped, 0, keepdims=False)
        stored = jnp.where(active, grad_in, current)
        results = lax.dynamic_update_index_in_dim(results, stored, clipped, 0)
        from_below = from_behind(grad_in, "section", -1)
        higher = from_behind(grad_in, "section", 1)
        incoming = jnp.where(mirror_id == 0, from_below, higher)
        return (incoming, kernel_acc, results)

    initial = (
        jnp.zeros((tile_rows, tile_width, channels), jnp.bfloat16),
        jnp.zeros((9 * channels, channels), jnp.float32),
        jnp.zeros((micros, tile_rows, tile_width, channels), jnp.bfloat16),
    )
    _, kernel_acc, results = lax.fori_loop(0, micros + sections - 1, backward, initial)
    share_rows = 9 * channels // strips
    own_share = lax.psum_scatter(kernel_acc, "strip", scatter_dimension=0, tiled=True)
    blocks = own_share.reshape(sections, share_rows * channels // sections)
    spread = lax.all_to_all(blocks, "section", split_axis=0, concat_axis=0, tiled=True)
    across = swapped(spread.astype(jnp.bfloat16), "mirror", 0).astype(spread.dtype)
    combined = spread + jnp.flip(across, 0)
    returned = lax.all_to_all(combined, "section", split_axis=0, concat_axis=0, tiled=True)
    summed_share = returned.reshape(share_rows, channels)
    factor = 1.0 / math.sqrt(2.0 * micros * tile_rows * strips * tile_width)
    kernel_grads = (summed_share * factor)[None, None]
    input_grads = results[None, None]
    return (input_grads, kernel_grads)


AXES = ("section", "strip", "mirror")


def folded(grad_top, acts, masks, kernels):
    sections = lax.axis_size("section")
    strips = lax.axis_size("strip")
    half = sections // 2
    section_id = lax.axis_index("section")
    strip_id = lax.axis_index("strip")
    mirror_id = lax.axis_index("mirror")
    replica = jnp.where(section_id >= half, 0, 1)
    major = mirror_id == replica
    depth = jnp.where(section_id >= half, sections - 1 - section_id, section_id)
    bf16 = jnp.bfloat16

    def flat(s, z, m):
        return (s * strips + z) * 2 + m

    def is_major(s, m):
        return m == (0 if s >= half else 1)

    cells = [(s, m) for s in range(sections) for m in range(2)]

    def permuted(block, target, wanted=lambda s, m: True):
        route = []
        for s, m in cells:
            if wanted(s, m):
                t, n = target(s, m)
                route.extend((flat(s, z, m), flat(t, z, n)) for z in range(strips))
        return lax.ppermute(block, AXES, route)

    def mirrored(block):
        return lax.ppermute(block, "mirror", [(0, 1), (1, 0)])

    def partnered(block, wanted=lambda s, m: True):
        return permuted(block, lambda s, m: (sections - 1 - s, 1 - m), wanted)

    def opposite(block):
        return permuted(block, lambda s, m: (sections - 1 - s, m))

    def stripped(block, step, wanted=lambda s, m: True):
        route = [
            (flat(s, z, m), flat(s, z ^ step, m))
            for s, m in cells
            if wanted(s, m)
            for z in range(strips)
        ]
        return lax.ppermute(block, AXES, route)

    def hopped(block, position):
        inner = [min(q, sections - 1 - q) for q in (position, position + 1)]
        swap = {inner[0]: inner[1], inner[1]: inner[0]}
        swap.update({sections - 1 - a: sections - 1 - b for a, b in list(swap.items())})
        return permuted(block, lambda s, m: (swap[s], m), lambda s, m: s in swap)

    even = strip_id % 2 == 0

    def rims(first, last):
        near = [(z, z + 1) for z in range(0, strips - 1, 2)]
        far = [(z, z + 1) for z in range(1, strips - 1, 2)]
        near, far = [pairs + [(b, a) for a, b in pairs] for pairs in (near, far)]
        from_near = lax.ppermute(jnp.where(even, last, first), "strip", near)
        from_far = lax.ppermute(jnp.where(even, first, last), "strip", far)
        return jnp.where(even, from_far, from_near), jnp.where(even, from_near, from_far)

    def across_strips(block):
        return jnp.concatenate([block, stripped(block, 1)])

    top_grads = grad_top[0]
    inputs_all = acts[0, 0]
    masks_int = masks[0, 0]
    micros, tile_rows, tile_width, channels = inputs_all.shape
    count = micros // 2
    pixels = tile_rows * tile_width
    rows = 9 * channels // strips

    mine = jnp.stack([top_grads[:count], masks_int[:count].astype(bf16)])
    own_data = jnp.stack([masks_int.astype(bf16), inputs_all])
    theirs = jnp.stack([top_grads[count:], masks_int[count:].astype(bf16)])
    received = mirrored(jnp.where(major, theirs, own_data[:, count:]))
    mine = jnp.where(major, mine, received)
    low, high = rims(mine[:, :, :sections], mine[:, :, tile_rows - sections :])
    top_ext, high_masks = jnp.concatenate([low, mine, high], axis=2)

    own_kernel = jnp.transpose(kernels[0, 0], (0, 1, 3, 2)).reshape(9 * channels, channels)
    other_kernel = mirrored(own_kernel)
    high_kernel = jnp.where(major, own_kernel, other_kernel)
    low_kernel = jnp.where(major, other_kernel, own_kernel)

    moved = opposite(jnp.where(major, received, own_data[:, :count]))
    given_inputs = mirrored(inputs_all[count:])
    high_inputs = jnp.where(major, inputs_all[:count], given_inputs)

    def later_rims():
        block = jnp.concatenate([moved, high_inputs[None]])
        first = jnp.concatenate([block[0, :, :half], block[1, :, :1], block[2, :, :1]], axis=1)
        end = tile_rows
        last = jnp.concatenate(
            [block[0, :, end - half :], block[1, :, end - 1 :], block[2, :, end - 1 :]], axis=1
        )
        low, high = rims(first, last)
        low_masks = jnp.concatenate([low[:, :half], block[0], high[:, :half]], axis=1)
        low_inputs = [low[:, half : half + 1], block[1], high[:, half : half + 1]]
        high_inputs_ext = [low[:, half + 1 :], block[2], high[:, half + 1 :]]
        inputs = jnp.concatenate(
            [jnp.concatenate(high_inputs_ext, axis=1), jnp.concatenate(low_inputs, axis=1)]
        )
        return low_masks, across_strips(inputs[None])

    column, upper_strip = strip_id % 2, strip_id // 2

    def unfolded(tall):
        wide = jnp.pad(tall, ((0, 0), (0, 0), (0, 0), (1, 1), (0, 0)))

        def tap(index):
            a, b = divmod(index, 3)
            return wide[:, :, a : a + tile_rows, b : b + tile_width]

        pieces = [
            jnp.where(column == 1, tap(first + 2), tap(first)) for first in (0, 1, 2, 4, 5, 6)
        ]
        joined = jnp.concatenate(pieces, axis=-1).reshape(2, 2, count * pixels, 6 * channels)
        return joined.swapaxes(0, 1).reshape(2, 2 * count * pixels, 6 * channels)

    def kept_rows(taps):
        start = column * (channels // 4)
        near = lax.dynamic_slice_in_dim(taps, start, rows)
        far = lax.dynamic_slice_in_dim(taps[3 * channels :], start + channels // 2, rows)
        return near, far

    def layer_back(grad_out, mask, kernel):
        height = grad_out.shape[0] - 2
        grad_pre = grad_out * mask
        padded = jnp.pad(grad_pre, ((0, 0), (1, 1), (0, 0)))
        patch = unfold(padded, height, tile_width, True)
        branch = jnp.dot(patch, kernel, preferred_element_type=jnp.float32)
        grad_in = grad_out[1:-1].astype(jnp.float32) + branch.reshape(height, tile_width, channels)
        return grad_in.astype(bf16), grad_pre

    grads = [top_ext[k] for k in range(count)]
    pres = [[None] * count for _ in range(sections)]
    outs = [[None] * count for _ in range(sections)]
    low_masks, inputs = later_rims()
    for position in range(sections):
        for k in range(count):
            lower = position >= half
            trim = position - half if lower else position
            mask = (low_masks if lower else high_masks)[k]
            mask = mask[trim : mask.shape[0] - trim]
            kernel = low_kernel if lower else high_kernel
            grad_in, grad_pre = layer_back(grads[k], mask, kernel)
            rim = sections - position
            pres[position][k] = grad_pre[rim : rim + tile_rows]
            outs[position][k] = grad_in[rim - 1 : rim - 1 + tile_rows]
            grads[k] = grad_in
            if position + 1 < sections and position + 1 != half:
                hop = hopped(grad_in, position)
                grads[k] = hop if position else jnp.where(depth == 0, grad_in, hop)

    def at_depth(pieces):
        chosen = pieces[0]
        for q in range(1, half):
            chosen = jnp.where(depth == q, pieces[q], chosen)
        return chosen

    def side(table, lower, k):
        return at_depth([table[sections - 1 - q if lower else q][k] for q in range(half)])

    results = [jnp.stack([side(outs, lower, k) for k in range(count)]) for lower in range(2)]
    given = mirrored(jnp.where(major, results[1], results[0]))
    kept = jnp.concatenate([results[0], given])
    returned = partnered(jnp.concatenate([given, results[1]]), lambda s, m: not is_major(s, m))
    input_grads = jnp.where(major, kept, returned)

    patches = unfolded(inputs)
    sums = []
    for lower in range(2):
        block = jnp.stack([side(pres, lower, k) for k in range(count)])[None]
        block = across_strips(block).reshape(-1, channels)
        own = lax.dot_general(
            patches[lower], block, (((0,), (0,)), ((), ())), preferred_element_type=jnp.float32
        )
        own = jnp.stack(kept_rows(own)).reshape(2, 2, rows // 2, channels)
        first, second = own[:, 0], own[:, 1]
        other = jnp.where(major, second, first).astype(bf16)
        own = jnp.where(major, first, second)
        own = own + mirrored(other).astype(jnp.float32)
        other = jnp.where(upper_strip == 0, own[1], own[0]).astype(bf16)
        own = jnp.where(upper_strip == 0, own[0], own[1])
        own = own + stripped(other, 2).astype(jnp.float32)
        sums.append(own + partnered(own.astype(bf16)).astype(jnp.float32))
    factor = 1.0 / math.sqrt(2.0 * micros * tile_rows * strips * tile_width)
    other = mirrored(jnp.where(major, sums[1], sums[0]).astype(bf16)).astype(jnp.float32)
    own = jnp.where(major, sums[0], sums[1])
    kernel_grads = jnp.where(
        major, jnp.concatenate([own, other]), jnp.concatenate([other, own])
    )
    kernel_grads = kernel_grads * factor
    return (input_grads[None, None], kernel_grads[None, None])


def shards(grad_top, acts, masks, kernels):
    sections = lax.axis_size("section")
    strips = lax.axis_size("strip")
    tile_rows, channels = acts.shape[3], acts.shape[5]
    paired = sections % 2 == 0 and acts.shape[2] % 2 == 0 and strips == 4
    if paired and sections <= tile_rows and 9 * channels % strips == 0:
        return folded(grad_top, acts, masks, kernels)
    return pipelined(grad_top, acts, masks, kernels)


def solution(mesh):
    return mapped(mesh)


def mapped(mesh):
    return jax.shard_map(
        shards,
        mesh=mesh,
        in_specs=(
            P("mirror", None, "strip", None, None),
            P("mirror", "section", None, "strip", None, None),
            P("mirror", "section", None, "strip", None, None),
            P("mirror", "section", None, None, None, None),
        ),
        out_specs=(
            P("mirror", "section", None, "strip", None, None),
            P("mirror", "section", "strip", None),
        ),
        check_vma=False,
    )
```

```python
import math

import jax
import jax.numpy as jnp
from jax import lax
from jax.sharding import PartitionSpec as P


def with_halo(block, sides, width):
    for axis, dim in sides:
        count = lax.axis_size(axis)
        forward = [(i, i + 1) for i in range(count - 1)]
        backward = [(target, source) for source, target in forward]
        low = lax.ppermute(
            lax.slice_in_dim(block, block.shape[dim] - width, None, axis=dim), axis, forward
        )
        high = lax.ppermute(lax.slice_in_dim(block, 0, width, axis=dim), axis, backward)
        block = jnp.concatenate([low, block, high], axis=dim)
    return block


def from_behind(block, axis, distance):
    devices = range(lax.axis_size(axis))
    route = [(i - distance, i) for i in devices if i - distance in devices]
    return lax.ppermute(block, axis, route)


def swapped(shard, axis, bit):
    return lax.ppermute(shard, axis, [(i, i ^ 1 << bit) for i in range(lax.axis_size(axis))])


def unfold(padded, height, tile_width, flipped):
    pieces = []
    for row_shift in range(3):
        for col_shift in range(3):
            if flipped:
                row_start = 2 - row_shift
                col_start = 2 - col_shift
            else:
                row_start = row_shift
                col_start = col_shift
            pieces.append(
                padded[row_start : row_start + height, col_start : col_start + tile_width]
            )
    stacked = jnp.concatenate(pieces, axis=-1)
    return stacked.reshape(height * tile_width, stacked.shape[-1])


def pipelined(grad_top, acts, masks, kernels):
    sections = lax.axis_size("section")
    strips = lax.axis_size("strip")
    section_id = lax.axis_index("section")
    mirror_id = lax.axis_index("mirror")
    layer_id = jnp.where(mirror_id == 0, section_id, sections - 1 - section_id)
    delay_ticks = sections - 1 - layer_id
    top_grads = grad_top[0]
    inputs_all = acts[0, 0]
    masks_all = masks[0, 0]
    kernel = kernels[0, 0]
    micros, tile_rows, tile_width, channels = inputs_all.shape
    kernel_t = jnp.transpose(kernel, (0, 1, 3, 2)).reshape(9 * channels, channels)
    width_pad = ((0, 0), (1, 1), (0, 0))

    def compute(operands):
        grad_rim, input_rim, grad_out, kernel_acc = operands
        grad_pre = grad_rim[1:-1]
        input_patch = unfold(jnp.pad(input_rim, width_pad), tile_rows, tile_width, False)
        grad_patch = unfold(jnp.pad(grad_rim, width_pad), tile_rows, tile_width, True)
        kernel_acc = kernel_acc + lax.dot_general(
            input_patch,
            grad_pre.reshape(tile_rows * tile_width, channels),
            (((0,), (0,)), ((), ())),
            preferred_element_type=jnp.float32,
        )
        branch = jnp.dot(grad_patch, kernel_t, preferred_element_type=jnp.float32)
        grad_in = grad_out.astype(jnp.float32) + branch.reshape(tile_rows, tile_width, channels)
        return (grad_in.astype(jnp.bfloat16), kernel_acc)

    def skipped(operands):
        return (jnp.zeros_like(operands[2]), operands[3])

    def backward(tick_id, carried):
        incoming, kernel_acc, results = carried
        micro_id = tick_id - delay_ticks
        active = jnp.logical_and(micro_id >= 0, micro_id < micros)
        clipped = jnp.clip(micro_id, 0, micros - 1)
        from_top = lax.dynamic_index_in_dim(top_grads, clipped, 0, keepdims=False)
        grad_out = jnp.where(layer_id == sections - 1, from_top, incoming)
        relu_mask = lax.dynamic_index_in_dim(masks_all, clipped, 0, keepdims=False)
        grad_pre = (grad_out.astype(jnp.float32) * relu_mask.astype(jnp.float32)).astype(
            jnp.bfloat16
        )
        inputs = lax.dynamic_index_in_dim(inputs_all, clipped, 0, keepdims=False)
        rimmed = with_halo(jnp.stack([grad_pre, inputs]), (("strip", 1),), 1)
        grad_rim = rimmed[0]
        input_rim = rimmed[1]
        grad_in, kernel_acc = lax.cond(
            active, compute, skipped, (grad_rim, input_rim, grad_out, kernel_acc)
        )
        current = lax.dynamic_index_in_dim(results, clipped, 0, keepdims=False)
        stored = jnp.where(active, grad_in, current)
        results = lax.dynamic_update_index_in_dim(results, stored, clipped, 0)
        from_below = from_behind(grad_in, "section", -1)
        higher = from_behind(grad_in, "section", 1)
        incoming = jnp.where(mirror_id == 0, from_below, higher)
        return (incoming, kernel_acc, results)

    initial = (
        jnp.zeros((tile_rows, tile_width, channels), jnp.bfloat16),
        jnp.zeros((9 * channels, channels), jnp.float32),
        jnp.zeros((micros, tile_rows, tile_width, channels), jnp.bfloat16),
    )
    _, kernel_acc, results = lax.fori_loop(0, micros + sections - 1, backward, initial)
    share_rows = 9 * channels // strips
    own_share = lax.psum_scatter(kernel_acc, "strip", scatter_dimension=0, tiled=True)
    blocks = own_share.reshape(sections, share_rows * channels // sections)
    spread = lax.all_to_all(blocks, "section", split_axis=0, concat_axis=0, tiled=True)
    across = swapped(spread.astype(jnp.bfloat16), "mirror", 0).astype(spread.dtype)
    combined = spread + jnp.flip(across, 0)
    returned = lax.all_to_all(combined, "section", split_axis=0, concat_axis=0, tiled=True)
    summed_share = returned.reshape(share_rows, channels)
    factor = 1.0 / math.sqrt(2.0 * micros * tile_rows * strips * tile_width)
    kernel_grads = (summed_share * factor)[None, None]
    input_grads = results[None, None]
    return (input_grads, kernel_grads)


AXES = ("section", "strip", "mirror")


def folded(grad_top, acts, masks, kernels):
    sections = lax.axis_size("section")
    strips = lax.axis_size("strip")
    half = sections // 2
    section_id = lax.axis_index("section")
    strip_id = lax.axis_index("strip")
    mirror_id = lax.axis_index("mirror")
    replica = jnp.where(section_id >= half, 0, 1)
    major = mirror_id == replica
    depth = jnp.where(section_id >= half, sections - 1 - section_id, section_id)
    bf16 = jnp.bfloat16

    def flat(s, z, m):
        return (s * strips + z) * 2 + m

    cells = [(s, m) for s in range(sections) for m in range(2)]

    def permuted(block, target, wanted=lambda s, m: True):
        route = []
        for s, m in cells:
            if wanted(s, m):
                t, n = target(s, m)
                route.extend((flat(s, z, m), flat(t, z, n)) for z in range(strips))
        return lax.ppermute(block, AXES, route)

    def mirrored(block):
        return lax.ppermute(block, "mirror", [(0, 1), (1, 0)])

    def partnered(block, wanted=lambda s, m: True):
        return permuted(block, lambda s, m: (sections - 1 - s, 1 - m), wanted)

    def opposite(block):
        return permuted(block, lambda s, m: (sections - 1 - s, m))

    def stripped(block, step, wanted=lambda s, m: True):
        route = [
            (flat(s, z, m), flat(s, z ^ step, m))
            for s, m in cells
            if wanted(s, m)
            for z in range(strips)
        ]
        return lax.ppermute(block, AXES, route)

    def hopped(block, position):
        inner = [min(q, sections - 1 - q) for q in (position, position + 1)]
        swap = {inner[0]: inner[1], inner[1]: inner[0]}
        swap.update({sections - 1 - a: sections - 1 - b for a, b in list(swap.items())})
        return permuted(block, lambda s, m: (swap[s], m), lambda s, m: s in swap)

    even = strip_id % 2 == 0

    def rims(first, last):
        from_near = lax.ppermute(
            jnp.where(even, last, first), "strip", [(z, z ^ 1) for z in range(strips)]
        )

        def far(s, z, m):
            other = z + 1 if z % 2 else z - 1
            return (s, other, m) if 0 <= other < strips else (s, z, 1 - m)

        route = [
            (flat(s, z, m), flat(*far(s, z, m))) for s, m in cells for z in range(strips)
        ]
        from_far = lax.ppermute(jnp.where(even, first, last), AXES, route)
        low, high = jnp.where(even, from_far, from_near), jnp.where(even, from_near, from_far)
        zero = jnp.zeros_like(low)
        return jnp.where(strip_id == 0, zero, low), jnp.where(strip_id == strips - 1, zero, high)

    def across_strips(block, step):
        return jnp.stack([block, stripped(block, step)])

    top_grads = grad_top[0]
    inputs_all = acts[0, 0]
    masks_int = masks[0, 0]
    micros, tile_rows, tile_width, channels = inputs_all.shape
    count = micros // 2
    pixels = tile_rows * tile_width
    rows = 9 * channels // strips

    mine = jnp.stack([top_grads[:count], masks_int[:count].astype(bf16)])
    own_data = jnp.stack([masks_int.astype(bf16), inputs_all])
    theirs = jnp.stack([top_grads[count:], masks_int[count:].astype(bf16)])
    received = mirrored(jnp.where(major, theirs, own_data[:, count:]))
    mine = jnp.where(major, mine, received)
    low, high = rims(mine[:, :, :sections], mine[:, :, tile_rows - sections :])
    top_ext, high_masks = jnp.concatenate([low, mine, high], axis=2)

    own_kernel = jnp.transpose(kernels[0, 0], (0, 1, 3, 2)).reshape(9 * channels, channels)
    other_kernel = mirrored(own_kernel)
    high_kernel = jnp.where(major, own_kernel, other_kernel)
    low_kernel = jnp.where(major, other_kernel, own_kernel)

    moved = opposite(jnp.where(major, received, own_data[:, :count]))
    given_inputs = mirrored(inputs_all[count:])
    high_inputs = jnp.where(major, inputs_all[:count], given_inputs)

    def later_rims():
        block = jnp.concatenate([moved, high_inputs[None]])
        first = jnp.concatenate([block[0, :, :half], block[1, :, :1], block[2, :, :1]], axis=1)
        end = tile_rows
        last = jnp.concatenate(
            [block[0, :, end - half :], block[1, :, end - 1 :], block[2, :, end - 1 :]], axis=1
        )
        low, high = rims(first, last)
        low_masks = jnp.concatenate([low[:, :half], block[0], high[:, :half]], axis=1)
        low_inputs = [low[:, half : half + 1], block[1], high[:, half : half + 1]]
        high_inputs_ext = [low[:, half + 1 :], block[2], high[:, half + 1 :]]
        inputs = [jnp.concatenate(high_inputs_ext, axis=1), jnp.concatenate(low_inputs, axis=1)]
        return low_masks, inputs

    column, upper_strip = strip_id % 2, strip_id // 2

    def unfolded(tall, lower):
        wide = jnp.pad(tall, ((0, 0), (0, 0), (0, 0), (1, 1), (0, 0)))

        def tap(index):
            a, b = divmod(index, 3)
            return wide[:, :, a : a + tile_rows, b : b + tile_width]

        taps, flag, step = (range(5), upper_strip, 4) if lower else ((0, 1, 2, 4, 5, 6), column, 2)
        pieces = [jnp.where(flag == 1, tap(first + step), tap(first)) for first in taps]
        return jnp.concatenate(pieces, axis=-1).reshape(2 * count * pixels, len(taps) * channels)

    def kept_rows(taps, lower):
        if lower:
            start = upper_strip * (channels // 2)
            far = lax.dynamic_slice_in_dim(taps, start + rows, rows)
        else:
            start = column * (channels // 4)
            far = lax.dynamic_slice_in_dim(taps[3 * channels :], start + channels // 2, rows)
        return lax.dynamic_slice_in_dim(taps, start, rows), far

    def layer_back(grad_out, mask, kernel):
        height = grad_out.shape[0] - 2
        grad_pre = grad_out * mask
        padded = jnp.pad(grad_pre, ((0, 0), (1, 1), (0, 0)))
        patch = unfold(padded, height, tile_width, True)
        branch = jnp.dot(patch, kernel, preferred_element_type=jnp.float32)
        grad_in = grad_out[1:-1].astype(jnp.float32) + branch.reshape(height, tile_width, channels)
        return grad_in.astype(bf16), grad_pre

    grads = [top_ext[k] for k in range(count)]
    pres = [[None] * count for _ in range(sections)]
    outs = [[None] * count for _ in range(sections)]
    low_masks, inputs = later_rims()
    for position in range(sections):
        for k in range(count):
            lower = position >= half
            trim = position - half if lower else position
            mask = (low_masks if lower else high_masks)[k]
            mask = mask[trim : mask.shape[0] - trim]
            kernel = low_kernel if lower else high_kernel
            grad_in, grad_pre = layer_back(grads[k], mask, kernel)
            rim = sections - position
            pres[position][k] = grad_pre[rim : rim + tile_rows]
            outs[position][k] = grad_in[rim - 1 : rim - 1 + tile_rows]
            grads[k] = grad_in
            if position + 1 < sections and position + 1 != half:
                hop = hopped(grad_in, position)
                grads[k] = hop if position else jnp.where(depth == 0, grad_in, hop)

    def at_depth(pieces):
        chosen = pieces[0]
        for q in range(1, half):
            chosen = jnp.where(depth == q, pieces[q], chosen)
        return chosen

    def side(table, lower, k):
        return at_depth([table[sections - 1 - q if lower else q][k] for q in range(half)])

    results = [jnp.stack([side(outs, lower, k) for k in range(count)]) for lower in range(2)]
    moved_back = opposite(results[1])
    given = mirrored(jnp.where(major, moved_back, results[0]))
    input_grads = jnp.concatenate([jnp.where(major, results[0], moved_back), given])

    sums = []
    for lower in range(2):
        gather_step, sum_step = (2, 1) if lower else (1, 2)
        tall = across_strips(inputs[lower], gather_step)
        patches = unfolded(tall, lower)
        block = jnp.stack([side(pres, lower, k) for k in range(count)])
        block = across_strips(block, gather_step).reshape(-1, channels)
        own = lax.dot_general(
            patches, block, (((0,), (0,)), ((), ())), preferred_element_type=jnp.float32
        )
        own = jnp.stack(kept_rows(own, lower)).reshape(2, 2, rows // 2, channels)
        first, second = own[:, 0], own[:, 1]
        other = jnp.where(major, second, first).astype(bf16)
        own = jnp.where(major, first, second)
        own = own + mirrored(other).astype(jnp.float32)
        place = column if lower else upper_strip
        other = jnp.where(place == 0, own[1], own[0]).astype(bf16)
        own = jnp.where(place == 0, own[0], own[1])
        own = own + stripped(other, sum_step).astype(jnp.float32)
        sums.append(own + partnered(own.astype(bf16)).astype(jnp.float32))
    factor = 1.0 / math.sqrt(2.0 * micros * tile_rows * strips * tile_width)
    other = mirrored(jnp.where(major, sums[1], sums[0]).astype(bf16)).astype(jnp.float32)
    own = jnp.where(major, sums[0], sums[1])
    kernel_grads = jnp.where(
        major, jnp.concatenate([own, other]), jnp.concatenate([other, own])
    )
    kernel_grads = kernel_grads * factor
    return (input_grads[None, None], kernel_grads[None, None])


def shards(grad_top, acts, masks, kernels):
    sections = lax.axis_size("section")
    strips = lax.axis_size("strip")
    tile_rows, channels = acts.shape[3], acts.shape[5]
    paired = sections % 2 == 0 and acts.shape[2] % 2 == 0 and strips == 4
    if paired and sections <= tile_rows and 9 * channels % strips == 0:
        return folded(grad_top, acts, masks, kernels)
    return pipelined(grad_top, acts, masks, kernels)


def solution(mesh):
    return mapped(mesh)


def mapped(mesh):
    return jax.shard_map(
        shards,
        mesh=mesh,
        in_specs=(
            P("mirror", None, "strip", None, None),
            P("mirror", "section", None, "strip", None, None),
            P("mirror", "section", None, "strip", None, None),
            P("mirror", "section", None, None, None, None),
        ),
        out_specs=(
            P("mirror", "section", None, "strip", None, None),
            P("mirror", "section", "strip", None),
        ),
        check_vma=False,
    )
```

```python
import math

import jax
import jax.numpy as jnp
from jax import lax
from jax.sharding import PartitionSpec as P


def with_halo(block, sides, width):
    for axis, dim in sides:
        count = lax.axis_size(axis)
        forward = [(i, i + 1) for i in range(count - 1)]
        backward = [(target, source) for source, target in forward]
        low = lax.ppermute(
            lax.slice_in_dim(block, block.shape[dim] - width, None, axis=dim), axis, forward
        )
        high = lax.ppermute(lax.slice_in_dim(block, 0, width, axis=dim), axis, backward)
        block = jnp.concatenate([low, block, high], axis=dim)
    return block


def from_behind(block, axis, distance):
    devices = range(lax.axis_size(axis))
    route = [(i - distance, i) for i in devices if i - distance in devices]
    return lax.ppermute(block, axis, route)


def swapped(shard, axis, bit):
    return lax.ppermute(shard, axis, [(i, i ^ 1 << bit) for i in range(lax.axis_size(axis))])


def unfold(padded, height, tile_width, flipped):
    pieces = []
    for row_shift in range(3):
        for col_shift in range(3):
            if flipped:
                row_start = 2 - row_shift
                col_start = 2 - col_shift
            else:
                row_start = row_shift
                col_start = col_shift
            pieces.append(
                padded[row_start : row_start + height, col_start : col_start + tile_width]
            )
    stacked = jnp.concatenate(pieces, axis=-1)
    return stacked.reshape(height * tile_width, stacked.shape[-1])


def pipelined(grad_top, acts, masks, kernels):
    sections = lax.axis_size("section")
    strips = lax.axis_size("strip")
    section_id = lax.axis_index("section")
    mirror_id = lax.axis_index("mirror")
    layer_id = jnp.where(mirror_id == 0, section_id, sections - 1 - section_id)
    delay_ticks = sections - 1 - layer_id
    top_grads = grad_top[0]
    inputs_all = acts[0, 0]
    masks_all = masks[0, 0]
    kernel = kernels[0, 0]
    micros, tile_rows, tile_width, channels = inputs_all.shape
    kernel_t = jnp.transpose(kernel, (0, 1, 3, 2)).reshape(9 * channels, channels)
    width_pad = ((0, 0), (1, 1), (0, 0))

    def compute(operands):
        grad_rim, input_rim, grad_out, kernel_acc = operands
        grad_pre = grad_rim[1:-1]
        input_patch = unfold(jnp.pad(input_rim, width_pad), tile_rows, tile_width, False)
        grad_patch = unfold(jnp.pad(grad_rim, width_pad), tile_rows, tile_width, True)
        kernel_acc = kernel_acc + lax.dot_general(
            input_patch,
            grad_pre.reshape(tile_rows * tile_width, channels),
            (((0,), (0,)), ((), ())),
            preferred_element_type=jnp.float32,
        )
        branch = jnp.dot(grad_patch, kernel_t, preferred_element_type=jnp.float32)
        grad_in = grad_out.astype(jnp.float32) + branch.reshape(tile_rows, tile_width, channels)
        return (grad_in.astype(jnp.bfloat16), kernel_acc)

    def skipped(operands):
        return (jnp.zeros_like(operands[2]), operands[3])

    def backward(tick_id, carried):
        incoming, kernel_acc, results = carried
        micro_id = tick_id - delay_ticks
        active = jnp.logical_and(micro_id >= 0, micro_id < micros)
        clipped = jnp.clip(micro_id, 0, micros - 1)
        from_top = lax.dynamic_index_in_dim(top_grads, clipped, 0, keepdims=False)
        grad_out = jnp.where(layer_id == sections - 1, from_top, incoming)
        relu_mask = lax.dynamic_index_in_dim(masks_all, clipped, 0, keepdims=False)
        grad_pre = (grad_out.astype(jnp.float32) * relu_mask.astype(jnp.float32)).astype(
            jnp.bfloat16
        )
        inputs = lax.dynamic_index_in_dim(inputs_all, clipped, 0, keepdims=False)
        rimmed = with_halo(jnp.stack([grad_pre, inputs]), (("strip", 1),), 1)
        grad_rim = rimmed[0]
        input_rim = rimmed[1]
        grad_in, kernel_acc = lax.cond(
            active, compute, skipped, (grad_rim, input_rim, grad_out, kernel_acc)
        )
        current = lax.dynamic_index_in_dim(results, clipped, 0, keepdims=False)
        stored = jnp.where(active, grad_in, current)
        results = lax.dynamic_update_index_in_dim(results, stored, clipped, 0)
        from_below = from_behind(grad_in, "section", -1)
        higher = from_behind(grad_in, "section", 1)
        incoming = jnp.where(mirror_id == 0, from_below, higher)
        return (incoming, kernel_acc, results)

    initial = (
        jnp.zeros((tile_rows, tile_width, channels), jnp.bfloat16),
        jnp.zeros((9 * channels, channels), jnp.float32),
        jnp.zeros((micros, tile_rows, tile_width, channels), jnp.bfloat16),
    )
    _, kernel_acc, results = lax.fori_loop(0, micros + sections - 1, backward, initial)
    share_rows = 9 * channels // strips
    own_share = lax.psum_scatter(kernel_acc, "strip", scatter_dimension=0, tiled=True)
    blocks = own_share.reshape(sections, share_rows * channels // sections)
    spread = lax.all_to_all(blocks, "section", split_axis=0, concat_axis=0, tiled=True)
    across = swapped(spread.astype(jnp.bfloat16), "mirror", 0).astype(spread.dtype)
    combined = spread + jnp.flip(across, 0)
    returned = lax.all_to_all(combined, "section", split_axis=0, concat_axis=0, tiled=True)
    summed_share = returned.reshape(share_rows, channels)
    factor = 1.0 / math.sqrt(2.0 * micros * tile_rows * strips * tile_width)
    kernel_grads = (summed_share * factor)[None, None]
    input_grads = results[None, None]
    return (input_grads, kernel_grads)


AXES = ("section", "strip", "mirror")


def folded(grad_top, acts, masks, kernels):
    sections = lax.axis_size("section")
    strips = lax.axis_size("strip")
    half = sections // 2
    section_id = lax.axis_index("section")
    strip_id = lax.axis_index("strip")
    mirror_id = lax.axis_index("mirror")
    replica = jnp.where(section_id >= half, 0, 1)
    major = mirror_id == replica
    depth = jnp.where(section_id >= half, sections - 1 - section_id, section_id)
    bf16 = jnp.bfloat16

    def flat(s, z, m):
        return (s * strips + z) * 2 + m

    cells = [(s, m) for s in range(sections) for m in range(2)]

    def permuted(block, target, wanted=lambda s, m: True):
        route = []
        for s, m in cells:
            if wanted(s, m):
                t, n = target(s, m)
                route.extend((flat(s, z, m), flat(t, z, n)) for z in range(strips))
        return lax.ppermute(block, AXES, route)

    def mirrored(block):
        return lax.ppermute(block, "mirror", [(0, 1), (1, 0)])

    def partnered(block, wanted=lambda s, m: True):
        return permuted(block, lambda s, m: (sections - 1 - s, 1 - m), wanted)

    def opposite(block):
        return permuted(block, lambda s, m: (sections - 1 - s, m))

    def stripped(block, step, wanted=lambda s, m: True):
        route = [
            (flat(s, z, m), flat(s, z ^ step, m))
            for s, m in cells
            if wanted(s, m)
            for z in range(strips)
        ]
        return lax.ppermute(block, AXES, route)

    def hopped(block, position):
        inner = [min(q, sections - 1 - q) for q in (position, position + 1)]
        swap = {inner[0]: inner[1], inner[1]: inner[0]}
        swap.update({sections - 1 - a: sections - 1 - b for a, b in list(swap.items())})
        return permuted(block, lambda s, m: (swap[s], m), lambda s, m: s in swap)

    even = strip_id % 2 == 0

    def rims(first, last):
        from_near = lax.ppermute(
            jnp.where(even, last, first), "strip", [(z, z ^ 1) for z in range(strips)]
        )

        def far(s, z, m):
            other = z + 1 if z % 2 else z - 1
            return (s, other, m) if 0 <= other < strips else (s, z, 1 - m)

        route = [
            (flat(s, z, m), flat(*far(s, z, m))) for s, m in cells for z in range(strips)
        ]
        from_far = lax.ppermute(jnp.where(even, first, last), AXES, route)
        low, high = jnp.where(even, from_far, from_near), jnp.where(even, from_near, from_far)
        zero = jnp.zeros_like(low)
        return jnp.where(strip_id == 0, zero, low), jnp.where(strip_id == strips - 1, zero, high)

    def across_strips(block, step):
        return jnp.stack([block, stripped(block, step)])

    top_grads = grad_top[0]
    inputs_all = acts[0, 0]
    masks_int = masks[0, 0]
    micros, tile_rows, tile_width, channels = inputs_all.shape
    count = micros // 2
    pixels = tile_rows * tile_width
    rows = 9 * channels // strips

    mine = jnp.stack([top_grads[:count], masks_int[:count].astype(bf16)])
    own_data = jnp.stack([masks_int.astype(bf16), inputs_all])
    theirs = jnp.stack([top_grads[count:], masks_int[count:].astype(bf16)])
    received = mirrored(jnp.where(major, theirs, own_data[:, count:]))
    mine = jnp.where(major, mine, received)
    low, high = rims(mine[:, :, :sections], mine[:, :, tile_rows - sections :])
    top_ext, high_masks = jnp.concatenate([low, mine, high], axis=2)

    own_kernel = kernels[0, 0]
    other_kernel = mirrored(own_kernel)

    def transposed(kernel):
        return jnp.transpose(kernel, (0, 1, 3, 2)).reshape(9 * channels, channels)

    high_kernel = transposed(jnp.where(major, own_kernel, other_kernel))
    low_kernel = transposed(jnp.where(major, other_kernel, own_kernel))

    moved = opposite(jnp.where(major, received, own_data[:, :count]))
    given_inputs = mirrored(inputs_all[count:])
    high_inputs = jnp.where(major, inputs_all[:count], given_inputs)

    def later_rims():
        block = jnp.concatenate([moved, high_inputs[None]])
        first = jnp.concatenate([block[0, :, :half], block[1, :, :1], block[2, :, :1]], axis=1)
        end = tile_rows
        last = jnp.concatenate(
            [block[0, :, end - half :], block[1, :, end - 1 :], block[2, :, end - 1 :]], axis=1
        )
        low, high = rims(first, last)
        low_masks = jnp.concatenate([low[:, :half], block[0], high[:, :half]], axis=1)
        low_inputs = [low[:, half : half + 1], block[1], high[:, half : half + 1]]
        high_inputs_ext = [low[:, half + 1 :], block[2], high[:, half + 1 :]]
        inputs = [jnp.concatenate(high_inputs_ext, axis=1), jnp.concatenate(low_inputs, axis=1)]
        return low_masks, inputs

    column, upper_strip = strip_id % 2, strip_id // 2

    def unfolded(tall, lower):
        wide = jnp.pad(tall, ((0, 0), (0, 0), (0, 0), (1, 1), (0, 0)))

        def tap(index):
            a, b = divmod(index, 3)
            return wide[:, :, a : a + tile_rows, b : b + tile_width]

        taps, flag, step = (range(5), upper_strip, 4) if lower else ((0, 1, 2, 4, 5, 6), column, 2)
        pieces = [jnp.where(flag == 1, tap(first + step), tap(first)) for first in taps]
        return jnp.concatenate(pieces, axis=-1).reshape(2 * count * pixels, len(taps) * channels)

    def kept_rows(taps, lower):
        if lower:
            start = upper_strip * (channels // 2)
            far = lax.dynamic_slice_in_dim(taps, start + rows, rows)
        else:
            start = column * (channels // 4)
            far = lax.dynamic_slice_in_dim(taps[3 * channels :], start + channels // 2, rows)
        return lax.dynamic_slice_in_dim(taps, start, rows), far

    def layer_back(grad_out, mask, kernel):
        height = grad_out.shape[1] - 2
        grad_pre = grad_out * mask
        padded = jnp.pad(grad_pre, ((0, 0), (0, 0), (1, 1), (0, 0)))
        patch = jnp.concatenate([unfold(one, height, tile_width, True) for one in padded])
        branch = jnp.dot(patch, kernel, preferred_element_type=jnp.float32)
        centre = grad_out[:, 1:-1]
        grad_in = centre.astype(jnp.float32) + branch.reshape(centre.shape)
        return grad_in.astype(bf16), grad_pre

    grads = top_ext
    low_masks, inputs = later_rims()
    pres, outs = [], []
    for position in range(sections):
        lower = position >= half
        trim = position - half if lower else position
        mask = low_masks if lower else high_masks
        mask = mask[:, trim : mask.shape[1] - trim]
        kernel = low_kernel if lower else high_kernel
        grad_in, grad_pre = layer_back(grads, mask, kernel)
        rim = sections - position
        pres.append(grad_pre[:, rim : rim + tile_rows])
        outs.append(grad_in[:, rim - 1 : rim - 1 + tile_rows])
        grads = grad_in
        if position + 1 < sections and position + 1 != half:
            hop = hopped(grad_in, position)
            grads = jnp.where(depth <= position, grad_in, hop) if position + 1 < half else hop

    def at_depth(pieces):
        chosen = pieces[0]
        for q in range(1, half):
            chosen = jnp.where(depth == q, pieces[q], chosen)
        return chosen

    def side(table, lower):
        return at_depth([table[sections - 1 - q if lower else q] for q in range(half)])

    results = [side(outs, lower) for lower in range(2)]
    moved_back = opposite(results[1])
    given = mirrored(jnp.where(major, moved_back, results[0]))
    input_grads = jnp.concatenate([jnp.where(major, results[0], moved_back), given])

    sums = []
    for lower in range(2):
        gather_step, sum_step = (2, 1) if lower else (1, 2)
        tall = across_strips(inputs[lower], gather_step)
        patches = unfolded(tall, lower)
        block = side(pres, lower)
        block = across_strips(block, gather_step).reshape(-1, channels)
        own = lax.dot_general(
            patches, block, (((0,), (0,)), ((), ())), preferred_element_type=jnp.float32
        )
        own = jnp.stack(kept_rows(own, lower)).reshape(2, 2, rows // 2, channels)
        first, second = own[:, 0], own[:, 1]
        other = jnp.where(major, second, first).astype(bf16)
        own = jnp.where(major, first, second)
        own = own + mirrored(other).astype(jnp.float32)
        place = column if lower else upper_strip
        other = jnp.where(place == 0, own[1], own[0]).astype(bf16)
        own = jnp.where(place == 0, own[0], own[1])
        own = own + stripped(other, sum_step).astype(jnp.float32)
        sums.append(own + partnered(own.astype(bf16)).astype(jnp.float32))
    factor = 1.0 / math.sqrt(2.0 * micros * tile_rows * strips * tile_width)
    other = mirrored(jnp.where(major, sums[1], sums[0]).astype(bf16)).astype(jnp.float32)
    own = jnp.where(major, sums[0], sums[1])
    kernel_grads = jnp.where(
        major, jnp.concatenate([own, other]), jnp.concatenate([other, own])
    )
    kernel_grads = kernel_grads * factor
    return (input_grads[None, None], kernel_grads[None, None])


def shards(grad_top, acts, masks, kernels):
    sections = lax.axis_size("section")
    strips = lax.axis_size("strip")
    tile_rows, channels = acts.shape[3], acts.shape[5]
    paired = sections % 2 == 0 and acts.shape[2] % 2 == 0 and strips == 4
    if paired and sections <= tile_rows and 9 * channels % strips == 0:
        return folded(grad_top, acts, masks, kernels)
    return pipelined(grad_top, acts, masks, kernels)


def solution(mesh):
    return mapped(mesh)


def mapped(mesh):
    return jax.shard_map(
        shards,
        mesh=mesh,
        in_specs=(
            P("mirror", None, "strip", None, None),
            P("mirror", "section", None, "strip", None, None),
            P("mirror", "section", None, "strip", None, None),
            P("mirror", "section", None, None, None, None),
        ),
        out_specs=(
            P("mirror", "section", None, "strip", None, None),
            P("mirror", "section", "strip", None),
        ),
        check_vma=False,
    )
```
